32 devices in a mesh: dp: 8 (over y, x, core), fsdp: 4 (over z).
Axes of the slice: x: 2, y: 2, z: 4, core: 2. Of those that a mesh axis runs over, the one named last changes fastest.
Arguments:
- tokens: bfloat16 [16384, 1024], P(('dp', 'fsdp')), may hold values from -20 to 20
- w_qkv: bfloat16 [1024, 3072], P('fsdp'), may hold values from -0.1875 to 0.1875
- w_out: bfloat16 [1024, 1024], P('fsdp'), may hold values from -0.1875 to 0.1875
- doc_blocks: int32 [32, 4], P(('dp', 'fsdp')), may hold values from 0 to 1, never falling along the last dimension, each value on 1 to 3 neighbouring positions
- cotangent: bfloat16 [16384, 1024], P(('dp', 'fsdp')), may hold values from -6 to 6
Outputs:
- output: bfloat16 [16384, 1024], P(('dp', 'fsdp'))
- grad_tokens: bfloat16 [16384, 1024], P(('dp', 'fsdp'))
- grad_w_qkv: float32 [1024, 3072], P('fsdp')
- grad_w_out: float32 [1024, 1024], P('fsdp')
The draws below stay inside these ranges and needn't reach their ends.
Inputs may be any that keep to these rules, and one draw needn't show every extreme that they name: `doc_blocks`: ids never fall along a sequence; each of the 2 documents of a sequence covers 1 to 3 blocks.
All inputs are finite; a program needn't handle non-finite values.
Results may differ from the reference program's by a relative error of at most 0.012.
Values may be sent and summed in bfloat16 or wider, within the bound.
A program may use at most 128 MiB of HBM per device.

```python
import math
import jax
import jax.numpy as jnp
import numpy as np
from jax import lax

D = 1024
H = 8
HD = 128
TOK_DEV = 512
HW = 1024
NB = 4
DOCS = 2
MOST = 3
SEQS = 32
TOKENS = 16384


def draw_tokens(key, part):
    first = jax.random.fold_in(key, 0)
    values = jnp.clip(jax.random.normal(first, (TOKENS, D), jnp.float32), -6.0, 6.0)
    return values.astype(jnp.bfloat16)


def with_spikes(drawn, stream_key, source, target, shards_of, factor):
    owner, partner = [(jnp.arange(drawn.shape[dim]) // (drawn.shape[dim] // shards_of)).reshape([-1 if axis == dim else 1 for axis in range(drawn.ndim)]) for dim in (source, target)]
    chosen = jax.random.permutation(stream_key, shards_of)[partner]
    strong = (owner == chosen) | (owner == (partner + shards_of // 2) % shards_of)
    return jnp.where(strong, factor * drawn, drawn)


def steps_of(rng, dims, shards, least, top_value):
    level, own = 1.0, jax.random.fold_in(rng, 6)
    for dim, parts in shards:
        draws = jnp.exp(jax.random.uniform(jax.random.fold_in(own, dim), (parts,), jnp.float32, least / len(shards), top_value / len(shards)))
        level = level * jnp.repeat(draws, dims[dim] // parts).reshape([-1 if axis == dim else 1 for axis in range(len(dims))])
    return level


def length_profile(amount, total, reach, slope):
    portions = [(1 << 20) // math.isqrt(rank ** slope) + 1 for rank in range(2, amount + 1)]
    rest, given = total - reach - (amount - 1), [1] * (amount - 1)
    while rest > 0:
        candidates = [i for i in range(amount - 1) if given[i] < reach]
        pool, left = sum([portions[i] for i in candidates]), rest
        for i in candidates:
            extra = min(reach - given[i], max(1, left * portions[i] // pool), rest)
            given[i] = given[i] + extra
            rest = rest - extra
    return np.array([reach] + given)


def uneven_parts(key, number_of, total, reach, skew):
    if number_of == 2:
        one = jax.random.randint(key, (), max(1, total - reach), min(reach, total - 1) + 1)
        return jnp.stack([one, total - one])
    lengths = jnp.asarray(length_profile(number_of, total, reach, skew), jnp.int32)
    pairs = (number_of - 1) // 2
    giver, receiver = lengths[1:1 + 2 * pairs:2], lengths[2:2 + 2 * pairs:2]
    slack = jnp.minimum(giver - 1, reach - receiver)
    passed = jax.random.randint(jax.random.fold_in(key, 1), (pairs,), 0, 1 << 20) % (slack + 1)
    lengths = lengths.at[1:1 + 2 * pairs:2].set(giver - passed).at[2:2 + 2 * pairs:2].set(receiver + passed)
    return lengths[jax.random.permutation(jax.random.fold_in(key, 2), number_of)]


def centred(stream_key, shape, scale, reach, cuts=(), held_as=jnp.bfloat16):
    loudness = steps_of(stream_key, shape, cuts, -0.22, 0.18) if cuts else 1.0
    drawn = jax.random.normal(stream_key, shape, jnp.float32) * scale * loudness
    return jnp.minimum(jnp.maximum(drawn, -reach), reach).astype(held_as)


def noise_with(key, extent, spread, most, cuts, heavy, kind=jnp.bfloat16):
    entries = spread * jax.random.normal(key, extent, jnp.float32)
    if cuts:
        entries = entries * steps_of(key, extent, cuts, -0.22, 0.18)
    return jnp.clip(with_spikes(entries, jax.random.fold_in(key, 3), *heavy), -most, most).astype(kind)


def setup_inputs(seed: int = 0) -> dict:
    keys = jax.random.split(jax.random.key(seed), 6)
    tokens = draw_tokens(jax.random.fold_in(keys[5], 71), 0)
    w_qkv = centred(keys[1], (D, 3 * HW), D ** -0.5, 0.1875, ((0, 4),))
    w_out = centred(keys[2], (D, HW), HW ** -0.5, 0.1875, ((0, 4),))
    doc_blocks = jax.vmap(lambda own: jnp.searchsorted(jnp.cumsum(uneven_parts(own, DOCS, NB, MOST, 0)), jnp.arange(NB), side="right"))(jax.random.split(keys[3], SEQS)).reshape((SEQS, NB)).astype(jnp.int32)
    cotangent = noise_with(keys[4], (TOKENS, D), 1.0, 6.0, ((0, 32),), (0, 1, 32, 2.75))
    return {"tokens": tokens, "w_qkv": w_qkv, "w_out": w_out, "doc_blocks": doc_blocks, "cotangent": cotangent}


NEG_FILL = -1e+30

def row_mask(doc_ids, row_count):
    block_len = row_count // doc_ids.shape[0]
    doc_rows = jnp.repeat(doc_ids, block_len, total_repeat_length=row_count)
    position = jnp.arange(row_count, dtype=jnp.int32)
    causal = position[None, :] <= position[:, None]
    return causal & (doc_rows[None, :] == doc_rows[:, None])

def split_heads(matrix, head_count):
    return matrix.reshape(matrix.shape[0], head_count, matrix.shape[1] // head_count).astype(jnp.float32)

def attend_forward(query_rows, key_rows, value_rows, allowed, head_count):
    row_count = query_rows.shape[0]
    query_heads = split_heads(query_rows, head_count)
    key_heads = split_heads(key_rows, head_count)
    value_heads = split_heads(value_rows, head_count)
    score_scale = query_heads.shape[2] ** (-0.5)
    scores = jnp.einsum('qhd,khd->hqk', query_heads, key_heads, precision=lax.Precision.HIGHEST) * score_scale
    scores = jnp.where(allowed[None], scores, NEG_FILL)
    highest = lax.optimization_barrier(jnp.max(scores, axis=-1, keepdims=True))
    expvals = jnp.exp(scores - highest)
    attn_probs = expvals / lax.optimization_barrier(jnp.sum(expvals, axis=-1, keepdims=True))
    probs_half = attn_probs.astype(jnp.bfloat16)
    mixed = jnp.einsum('hqk,khd->qhd', probs_half.astype(jnp.float32), value_heads, precision=lax.Precision.HIGHEST)
    return (mixed.astype(jnp.bfloat16).reshape(row_count, -1), attn_probs, probs_half)

def attend_backward(query_rows, key_rows, value_rows, attn_probs, probs_half, grad_mixed, head_count):
    row_count = query_rows.shape[0]
    query_heads = split_heads(query_rows, head_count)
    key_heads = split_heads(key_rows, head_count)
    value_heads = split_heads(value_rows, head_count)
    grad_heads = split_heads(grad_mixed, head_count)
    score_scale = query_heads.shape[2] ** (-0.5)
    grad_probs = jnp.einsum('qhd,khd->hqk', grad_heads, value_heads, precision=lax.Precision.HIGHEST)
    grad_values = jnp.einsum('hqk,qhd->khd', probs_half.astype(jnp.float32), grad_heads, precision=lax.Precision.HIGHEST)
    inner = lax.optimization_barrier(jnp.sum(attn_probs * grad_probs, axis=-1, keepdims=True))
    grad_scores = (attn_probs * (grad_probs - inner)).astype(jnp.bfloat16).astype(jnp.float32)
    grad_queries = jnp.einsum('hqk,khd->qhd', grad_scores, key_heads, precision=lax.Precision.HIGHEST) * score_scale
    grad_keys = jnp.einsum('hqk,qhd->khd', grad_scores, query_heads, precision=lax.Precision.HIGHEST) * score_scale
    pieces_list = [grad_queries, grad_keys, grad_values]
    return jnp.concatenate([p.astype(jnp.bfloat16).reshape(row_count, -1) for p in pieces_list], axis=1)

def reference(tokens, w_qkv, w_out, doc_blocks, cotangent):
    seq_count = doc_blocks.shape[0]
    token_seqs = tokens.reshape(seq_count, TOK_DEV, D)
    grad_seqs = cotangent.reshape(seq_count, TOK_DEV, D)
    head_width = H * HD

    def one_sequence(carry, item):
        seq_rows, seq_grad, doc_ids = item
        allowed = row_mask(doc_ids, TOK_DEV)
        qkv = jnp.dot(seq_rows, w_qkv, preferred_element_type=jnp.float32).astype(jnp.bfloat16)
        query_rows = qkv[:, :head_width]
        key_rows = qkv[:, head_width:2 * head_width]
        value_rows = qkv[:, 2 * head_width:]
        mixed, attn_probs, probs_half = attend_forward(query_rows, key_rows, value_rows, allowed, H)
        output = jnp.dot(mixed, w_out.T, preferred_element_type=jnp.float32).astype(jnp.bfloat16)
        grad_mixed = jnp.dot(seq_grad, w_out, preferred_element_type=jnp.float32).astype(jnp.bfloat16)
        grad_qkv = attend_backward(query_rows, key_rows, value_rows, attn_probs, probs_half, grad_mixed, H)
        grad_tokens = jnp.dot(grad_qkv, w_qkv.T, preferred_element_type=jnp.float32).astype(jnp.bfloat16)
        sum_qkv = carry[0] + jnp.dot(seq_rows.T, grad_qkv, preferred_element_type=jnp.float32)
        sum_out = carry[1] + jnp.dot(seq_grad.T, mixed, preferred_element_type=jnp.float32)
        return ((sum_qkv, sum_out), (output, grad_tokens))
    start_sums = (jnp.zeros((D, 3 * head_width), jnp.float32), jnp.zeros((D, head_width), jnp.float32))
    sums_final, outputs = lax.scan(one_sequence, start_sums, (token_seqs, grad_seqs, doc_blocks))
    norm_factor = 1.0 / math.sqrt(TOKENS)
    output = outputs[0].reshape(TOKENS, D)
    grad_tokens = outputs[1].reshape(TOKENS, D)
    return (output, grad_tokens, sums_final[0] * norm_factor, sums_final[1] * norm_factor)
```

```python
import functools
import math

import jax
import jax.numpy as jnp
from jax import lax
from jax.experimental import pallas as pl
from jax.experimental.pallas import tpu as pltpu
from jax.sharding import PartitionSpec as P

H = 8


NEG_FILL = -1e30
CONTRACT_ROWS = (((0,), (0,)), ((), ()))
CONTRACT_COLS = (((1,), (1,)), ((), ()))


def row_mask(doc_ids, row_count):
    block_len = row_count // doc_ids.shape[0]
    doc_rows = jnp.repeat(doc_ids, block_len, total_repeat_length=row_count)
    position = jnp.arange(row_count, dtype=jnp.int32)
    causal = position[None, :] <= position[:, None]
    return causal & (doc_rows[None, :] == doc_rows[:, None])


def split_heads(matrix, head_count):
    return matrix.reshape(matrix.shape[0], head_count, matrix.shape[1] // head_count)


def attend_forward(query_rows, key_rows, value_rows, allowed, head_count):
    row_count = query_rows.shape[0]
    query_heads = split_heads(query_rows, head_count)
    key_heads = split_heads(key_rows, head_count)
    value_heads = split_heads(value_rows, head_count)
    score_scale = query_heads.shape[2] ** (-0.5)
    scores = (
        jnp.einsum("qhd,khd->hqk", query_heads, key_heads, preferred_element_type=jnp.float32)
        * score_scale
    )
    scores = jnp.where(allowed[None], scores, NEG_FILL)
    highest = jnp.max(scores, axis=-1, keepdims=True)
    expvals = jnp.exp(scores - highest)
    attn_probs = expvals / jnp.sum(expvals, axis=-1, keepdims=True)
    probs_half = attn_probs.astype(jnp.bfloat16)
    mixed = jnp.einsum("hqk,khd->qhd", probs_half, value_heads, preferred_element_type=jnp.float32)
    return (mixed.astype(jnp.bfloat16).reshape(row_count, -1), attn_probs, probs_half)


def attend_backward(
    query_rows, key_rows, value_rows, attn_probs, probs_half, grad_mixed, head_count
):
    row_count = query_rows.shape[0]
    query_heads = split_heads(query_rows, head_count)
    key_heads = split_heads(key_rows, head_count)
    value_heads = split_heads(value_rows, head_count)
    grad_heads = split_heads(grad_mixed, head_count)
    score_scale = query_heads.shape[2] ** (-0.5)
    grad_probs = jnp.einsum(
        "qhd,khd->hqk", grad_heads, value_heads, preferred_element_type=jnp.float32
    )
    grad_values = jnp.einsum(
        "hqk,qhd->khd", probs_half, grad_heads, preferred_element_type=jnp.float32
    )
    inner = jnp.sum(attn_probs * grad_probs, axis=-1, keepdims=True)
    grad_scores = (attn_probs * (grad_probs - inner)).astype(jnp.bfloat16)
    grad_queries = (
        jnp.einsum("hqk,khd->qhd", grad_scores, key_heads, preferred_element_type=jnp.float32)
        * score_scale
    )
    grad_keys = (
        jnp.einsum("hqk,qhd->khd", grad_scores, query_heads, preferred_element_type=jnp.float32)
        * score_scale
    )
    pieces_list = [grad_queries, grad_keys, grad_values]
    return jnp.concatenate(
        [p.astype(jnp.bfloat16).reshape(row_count, -1) for p in pieces_list], axis=1
    )


def body(tokens, w_qkv, w_out, doc_blocks, cotangent):
    row_count = tokens.shape[0]
    head_width = w_out.shape[1]
    head_count = H
    all_devices = lax.axis_size("dp") * lax.axis_size("fsdp")
    allowed = row_mask(doc_blocks[0], row_count)
    columns = tokens
    qkv = jnp.dot(
        columns,
        lax.all_gather(w_qkv, "fsdp", axis=0, tiled=True),
        preferred_element_type=jnp.float32,
    ).astype(jnp.bfloat16)
    query_rows = qkv[:, :head_width]
    key_rows = qkv[:, head_width : 2 * head_width]
    value_rows = qkv[:, 2 * head_width :]
    mixed, attn_probs, probs_half = attend_forward(
        query_rows, key_rows, value_rows, allowed, head_count
    )
    output = lax.dot_general(
        mixed,
        lax.all_gather(w_out, "fsdp", axis=0, tiled=True),
        CONTRACT_COLS,
        preferred_element_type=jnp.float32,
    )
    columns = cotangent
    grad_mixed = jnp.dot(
        columns,
        lax.all_gather(w_out, "fsdp", axis=0, tiled=True),
        preferred_element_type=jnp.float32,
    ).astype(jnp.bfloat16)
    output = output.astype(jnp.bfloat16)
    grad_qkv = attend_backward(
        query_rows, key_rows, value_rows, attn_probs, probs_half, grad_mixed, head_count
    )
    grad_tokens = lax.dot_general(
        grad_qkv,
        lax.all_gather(w_qkv, "fsdp", axis=0, tiled=True),
        CONTRACT_COLS,
        preferred_element_type=jnp.float32,
    )
    grad_tokens = grad_tokens.astype(jnp.bfloat16)
    first_term = lax.dot_general(
        tokens, grad_qkv, CONTRACT_ROWS, preferred_element_type=jnp.float32
    )
    second_term = lax.dot_general(
        cotangent, mixed, CONTRACT_ROWS, preferred_element_type=jnp.float32
    )
    partial_grad = lax.psum_scatter(
        jnp.concatenate([first_term, second_term], axis=1), "fsdp", scatter_dimension=0, tiled=True
    )
    summed = lax.psum(partial_grad, "dp")
    norm_factor = 1.0 / math.sqrt(row_count * all_devices)
    grad_w_qkv = summed[:, : 3 * head_width] * norm_factor
    grad_w_out = summed[:, 3 * head_width :] * norm_factor
    return (output, grad_tokens, grad_w_qkv, grad_w_out)


MESH = pl.DeviceIdType.MESH
CHUNKS = 4


class Place:
    def __init__(self, fsdp_size):
        self.d, self.f = lax.axis_index("dp"), lax.axis_index("fsdp")
        self.c = lax.rem(self.d, 2)
        chip = lax.div(self.d, 2)
        self.x, self.y = lax.rem(chip, 2), lax.div(chip, 2)
        self.dx = self.dp_of(self.y, 1 - self.x, self.c)
        self.dy = self.dp_of(1 - self.y, self.x, self.c)
        self.dd = self.dp_of(1 - self.y, 1 - self.x, self.c)
        self.dc = self.dp_of(self.y, self.x, 1 - self.c)
        self.n = fsdp_size

    def dp_of(self, y, x, c):
        return (y * 2 + x) * 2 + c

    def ahead(self, j):
        return lax.rem(self.f + j, self.n)

    def behind(self, j):
        return lax.rem(self.f + self.n - j, self.n)

    def barrier(self):
        sem = pltpu.get_barrier_semaphore()
        targets = [(self.dx, self.f), (self.dy, self.f), (self.dc, self.f)]
        targets += [(self.d, self.ahead(j)) for j in range(1, self.n)]
        for target in targets:
            pl.semaphore_signal(sem, inc=1, device_id=target, device_id_type=MESH)
        pl.semaphore_wait(sem, len(targets))


def remote(src, dst, send_sem, recv_sem, target):
    return pltpu.make_async_remote_copy(
        src_ref=src,
        dst_ref=dst,
        send_sem=send_sem,
        recv_sem=recv_sem,
        device_id=target,
        device_id_type=MESH,
    )


def gather_kernel(n, wq_ref, wo_ref, fq_ref, fo_ref, send, recv, local_sem):
    me = Place(n)
    rows = wq_ref.shape[0]
    share = rows // 8
    half = share // 2
    mine, whole = (wq_ref, wo_ref), (fq_ref, fo_ref)
    me.barrier()
    started = {}

    def span(a, f, d, first, count):
        start = pl.multiple_of(f * rows + d * share + first, half)
        return whole[a].at[pl.ds(start, count)]

    def push(a, kind, j, f, d, first, count, target):
        spot = span(a, f, d, first, count)
        source = spot
        if kind == 0:
            source = mine[a].at[pl.ds(pl.multiple_of(d * share, share), share)]
        slot = kind * (n - 1) + j - 1
        copy = remote(source, spot, send.at[a, slot], recv.at[a, slot], target)
        copy.start()
        started[a, kind, j] = copy

    for j in range(1, n):
        for a in range(2):
            push(a, 0, j, me.f, me.d, 0, share, (me.d, me.ahead(j)))
    locals_ = []
    for a in range(2):
        start = pl.multiple_of(me.f * rows, rows)
        copy = pltpu.make_async_copy(mine[a], whole[a].at[pl.ds(start, rows)], local_sem.at[a])
        copy.start()
        locals_.append(copy)

    for step in range(1, n + 2):
        for a in range(2):
            j = step
            if j < n:
                f = me.behind(j)
                started[a, 0, j].wait_recv()
                push(a, 1, j, f, me.d, 0, share, (me.dx, me.f))
                push(a, 2, j, f, me.d, 0, share, (me.dy, me.f))
                push(a, 5, j, f, me.d, 0, share, (me.dc, me.f))
            j = step - 1
            if 1 <= j < n:
                f = me.behind(j)
                started[a, 1, j].wait_recv()
                push(a, 3, j, f, me.dx, 0, half, (me.dy, me.f))
                push(a, 6, j, f, me.dx, 0, share, (me.dc, me.f))
                started[a, 2, j].wait_recv()
                push(a, 4, j, f, me.dy, half, half, (me.dx, me.f))
                push(a, 7, j, f, me.dy, 0, share, (me.dc, me.f))
            j = step - 2
            if 1 <= j < n:
                f = me.behind(j)
                started[a, 3, j].wait_recv()
                push(a, 8, j, f, me.dd, 0, half, (me.dc, me.f))
                started[a, 4, j].wait_recv()
                push(a, 9, j, f, me.dd, half, half, (me.dc, me.f))
    for (a, kind, j), copy in started.items():
        copy.wait_send()
        if kind >= 5:
            copy.wait_recv()
    for copy in locals_:
        copy.wait()


def gather_weights(n, w_qkv, w_out):
    vmem = pl.BlockSpec(memory_space=pltpu.VMEM)
    return pl.pallas_call(
        functools.partial(gather_kernel, n),
        out_shape=[
            jax.ShapeDtypeStruct((w.shape[0] * n, w.shape[1]), w.dtype) for w in (w_qkv, w_out)
        ],
        in_specs=[vmem, vmem],
        out_specs=[pl.BlockSpec(memory_space=pl.ANY)] * 2,
        scratch_shapes=[
            pltpu.SemaphoreType.DMA((2, 10 * (n - 1))),
            pltpu.SemaphoreType.DMA((2, 10 * (n - 1))),
            pltpu.SemaphoreType.DMA((2,)),
        ],
        compiler_params=pltpu.CompilerParams(collective_id=0, has_side_effects=True),
        name="gather_weights",
    )(w_qkv, w_out)


def add_half(left, right):
    return left.astype(jnp.float32) + right.astype(jnp.float32)


def reduce_kernel(n, first_ref, second_ref, out_ref, core_sum, pair_sum, plane_sum, z_terms, send, recv):
    me = Place(n)
    width = second_ref.shape[-1]
    share = second_ref.shape[-2]
    half = share // 2
    me.barrier()
    started = {}

    def source(k):
        if k == CHUNKS - 1:
            return second_ref, pl.ds(0, width)
        return first_ref, pl.ds(k * width, width)

    def push(k, kind, src, dst, target):
        copy = remote(src, dst, send.at[k, kind], recv.at[k, kind], target)
        copy.start()
        started[k, kind] = copy

    def columns(k):
        return pl.ds(k * width, width)

    def core_start(k):
        ref, cols = source(k)
        push(k, 0, ref.at[:, :, :, 1 - me.c, :, cols], core_sum.at[k], (me.dc, me.f))

    def stage_core(k):
        ref, cols = source(k)
        started[k, 0].wait_recv()

        def add(i, carry):
            f, y, x = lax.div(i, 4), lax.rem(lax.div(i, 2), 2), lax.rem(i, 2)
            total = add_half(ref[f, y, x, me.c, :, cols], core_sum[k, f, y, x])
            core_sum[k, f, y, x] = total.astype(jnp.bfloat16)
            return carry

        lax.fori_loop(0, n * 4, add, 0)
        if k % 2 == 0:
            push(k, 1, core_sum.at[k, :, :, 1 - me.x], pair_sum.at[k], (me.dx, me.f))
        else:
            push(k, 1, core_sum.at[k, :, 1 - me.y], pair_sum.at[k], (me.dy, me.f))

    def stage_pair(k):
        started[k, 1].wait_recv()

        def add(i, carry):
            f, other = lax.div(i, 2), lax.rem(i, 2)
            own = core_sum[k, f, other, me.x] if k % 2 == 0 else core_sum[k, f, me.y, other]
            pair_sum[k, f, other] = add_half(own, pair_sum[k, f, other]).astype(jnp.bfloat16)
            return carry

        lax.fori_loop(0, n * 2, add, 0)
        if k % 2 == 0:
            push(k, 2, pair_sum.at[k, :, 1 - me.y], plane_sum.at[k], (me.dy, me.f))
        else:
            push(k, 2, pair_sum.at[k, :, 1 - me.x], plane_sum.at[k], (me.dx, me.f))

    def stage_plane(k):
        started[k, 2].wait_recv()
        keep = me.y if k % 2 == 0 else me.x

        def add(f, carry):
            plane_sum[k, f] = add_half(pair_sum[k, f, keep], plane_sum[k, f]).astype(jnp.bfloat16)
            return carry

        lax.fori_loop(0, n, add, 0)
        for j in range(1, n):
            push(k, 2 + j, plane_sum.at[k, me.ahead(j)], z_terms.at[k, j - 1], (me.d, me.ahead(j)))

    base = 2 + n

    def stage_z(k):
        total = plane_sum[k, me.f].astype(jnp.float32)
        for j in range(1, n):
            started[k, 2 + j].wait_recv()
            total = total + z_terms[k, j - 1].astype(jnp.float32)
        out_ref[me.d, :, columns(k)] = total.astype(jnp.bfloat16)
        spot = out_ref.at[me.d, :, columns(k)]
        push(k, base, spot, spot, (me.dx, me.f))
        push(k, base + 1, spot, spot, (me.dy, me.f))
        push(k, base + 4, spot, spot, (me.dc, me.f))

    def stage_spread(k):
        started[k, base].wait_recv()
        spot = out_ref.at[me.dx, pl.ds(0, half), columns(k)]
        push(k, base + 2, spot, spot, (me.dy, me.f))
        spot = out_ref.at[me.dx, :, columns(k)]
        push(k, base + 5, spot, spot, (me.dc, me.f))
        started[k, base + 1].wait_recv()
        spot = out_ref.at[me.dy, pl.ds(half, half), columns(k)]
        push(k, base + 3, spot, spot, (me.dx, me.f))
        spot = out_ref.at[me.dy, :, columns(k)]
        push(k, base + 6, spot, spot, (me.dc, me.f))

    def stage_last(k):
        started[k, base + 2].wait_recv()
        spot = out_ref.at[me.dd, pl.ds(0, half), columns(k)]
        push(k, base + 7, spot, spot, (me.dc, me.f))
        started[k, base + 3].wait_recv()
        spot = out_ref.at[me.dd, pl.ds(half, half), columns(k)]
        push(k, base + 8, spot, spot, (me.dc, me.f))

    order = [CHUNKS - 1] + list(range(CHUNKS - 1))
    for k in order:
        core_start(k)
    stages = [stage_core, stage_pair, stage_plane, stage_z, stage_spread, stage_last]
    for step in range(CHUNKS + len(stages) - 1):
        for s in reversed(range(len(stages))):
            if 0 <= step - s < CHUNKS:
                stages[s](order[step - s])
    for (k, kind), copy in started.items():
        copy.wait_send()
        if kind >= base + 4:
            copy.wait_recv()


def reduce_grads(n, first_term, second_term):
    share = first_term.shape[0] // (n * 8)
    width = second_term.shape[1]
    kinds = 2 + n + 9
    views = [g.reshape(n, 2, 2, 2, share, g.shape[1]) for g in (first_term, second_term)]
    vmem = pl.BlockSpec(memory_space=pltpu.VMEM)
    return pl.pallas_call(
        functools.partial(reduce_kernel, n),
        out_shape=jax.ShapeDtypeStruct((8, share, CHUNKS * width), jnp.bfloat16),
        in_specs=[vmem, vmem],
        out_specs=vmem,
        scratch_shapes=[
            pltpu.VMEM((CHUNKS, n, 2, 2, share, width), jnp.bfloat16),
            pltpu.VMEM((CHUNKS, n, 2, share, width), jnp.bfloat16),
            pltpu.VMEM((CHUNKS, n, share, width), jnp.bfloat16),
            pltpu.VMEM((CHUNKS, n - 1, share, width), jnp.bfloat16),
            pltpu.SemaphoreType.DMA((CHUNKS, kinds)),
            pltpu.SemaphoreType.DMA((CHUNKS, kinds)),
        ],
        compiler_params=pltpu.CompilerParams(
            collective_id=1, has_side_effects=True, vmem_limit_bytes=48 << 20
        ),
        name="reduce_grads",
    )(*views)


def chip_body(tokens, w_qkv, w_out, doc_blocks, cotangent):
    row_count = tokens.shape[0]
    head_width = w_out.shape[1]
    n = lax.axis_size("fsdp")
    all_devices = lax.axis_size("dp") * n
    allowed = row_mask(doc_blocks[0], row_count)
    full_qkv, full_out = gather_weights(n, w_qkv, w_out)
    qkv = jnp.dot(tokens, full_qkv, preferred_element_type=jnp.float32).astype(jnp.bfloat16)
    query_rows = qkv[:, :head_width]
    key_rows = qkv[:, head_width : 2 * head_width]
    value_rows = qkv[:, 2 * head_width :]
    mixed, attn_probs, probs_half = attend_forward(query_rows, key_rows, value_rows, allowed, H)
    output = lax.dot_general(
        mixed, full_out, CONTRACT_COLS, preferred_element_type=jnp.float32
    ).astype(jnp.bfloat16)
    grad_mixed = jnp.dot(cotangent, full_out, preferred_element_type=jnp.float32)
    grad_mixed = grad_mixed.astype(jnp.bfloat16)
    grad_qkv = attend_backward(
        query_rows, key_rows, value_rows, attn_probs, probs_half, grad_mixed, H
    )
    grad_tokens = lax.dot_general(
        grad_qkv, full_qkv, CONTRACT_COLS, preferred_element_type=jnp.float32
    ).astype(jnp.bfloat16)
    first_term = lax.dot_general(
        tokens, grad_qkv, CONTRACT_ROWS, preferred_element_type=jnp.float32
    ).astype(jnp.bfloat16)
    second_term = lax.dot_general(
        cotangent, mixed, CONTRACT_ROWS, preferred_element_type=jnp.float32
    ).astype(jnp.bfloat16)
    summed = reduce_grads(n, first_term, second_term)
    summed = summed.reshape(w_out.shape[0], 4 * head_width).astype(jnp.float32)
    norm_factor = 1.0 / math.sqrt(row_count * all_devices)
    grad_w_qkv = summed[:, : 3 * head_width] * norm_factor
    grad_w_out = summed[:, 3 * head_width :] * norm_factor
    return (output, grad_tokens, grad_w_qkv, grad_w_out)


def solution(mesh):
    placed = (
        P(("dp", "fsdp"), None),
        P("fsdp", None),
        P("fsdp", None),
        P(("dp", "fsdp"), None),
        P(("dp", "fsdp"), None),
    )
    in_plane = mesh.shape["dp"] == 8 and mesh.shape["fsdp"] == 4
    return jax.shard_map(
        chip_body if in_plane else body,
        mesh=mesh,
        in_specs=placed,
        out_specs=(
            P(("dp", "fsdp"), None),
            P(("dp", "fsdp"), None),
            P("fsdp", None),
            P("fsdp", None),
        ),
        check_vma=False,
    )
```

```python
import functools
import math

import jax
import jax.numpy as jnp
from jax import lax
from jax.experimental import pallas as pl
from jax.experimental.pallas import tpu as pltpu
from jax.sharding import PartitionSpec as P

H = 8


NEG_FILL = -1e30
CONTRACT_ROWS = (((0,), (0,)), ((), ()))
CONTRACT_COLS = (((1,), (1,)), ((), ()))


def row_mask(doc_ids, row_count):
    block_len = row_count // doc_ids.shape[0]
    doc_rows = jnp.repeat(doc_ids, block_len, total_repeat_length=row_count)
    position = jnp.arange(row_count, dtype=jnp.int32)
    causal = position[None, :] <= position[:, None]
    return causal & (doc_rows[None, :] == doc_rows[:, None])


def split_heads(matrix, head_count):
    return matrix.reshape(matrix.shape[0], head_count, matrix.shape[1] // head_count)


def attend_forward(query_rows, key_rows, value_rows, allowed, head_count):
    row_count = query_rows.shape[0]
    query_heads = split_heads(query_rows, head_count)
    key_heads = split_heads(key_rows, head_count)
    value_heads = split_heads(value_rows, head_count)
    score_scale = query_heads.shape[2] ** (-0.5)
    scores = (
        jnp.einsum("qhd,khd->hqk", query_heads, key_heads, preferred_element_type=jnp.float32)
        * score_scale
    )
    scores = jnp.where(allowed[None], scores, NEG_FILL)
    highest = jnp.max(scores, axis=-1, keepdims=True)
    expvals = jnp.exp(scores - highest)
    attn_probs = expvals / jnp.sum(expvals, axis=-1, keepdims=True)
    probs_half = attn_probs.astype(jnp.bfloat16)
    mixed = jnp.einsum("hqk,khd->qhd", probs_half, value_heads, preferred_element_type=jnp.float32)
    return (mixed.astype(jnp.bfloat16).reshape(row_count, -1), attn_probs, probs_half)


def attend_backward(
    query_rows, key_rows, value_rows, attn_probs, probs_half, grad_mixed, head_count
):
    row_count = query_rows.shape[0]
    query_heads = split_heads(query_rows, head_count)
    key_heads = split_heads(key_rows, head_count)
    value_heads = split_heads(value_rows, head_count)
    grad_heads = split_heads(grad_mixed, head_count)
    score_scale = query_heads.shape[2] ** (-0.5)
    grad_probs = jnp.einsum(
        "qhd,khd->hqk", grad_heads, value_heads, preferred_element_type=jnp.float32
    )
    grad_values = jnp.einsum(
        "hqk,qhd->khd", probs_half, grad_heads, preferred_element_type=jnp.float32
    )
    inner = jnp.sum(attn_probs * grad_probs, axis=-1, keepdims=True)
    grad_scores = (attn_probs * (grad_probs - inner)).astype(jnp.bfloat16)
    grad_queries = (
        jnp.einsum("hqk,khd->qhd", grad_scores, key_heads, preferred_element_type=jnp.float32)
        * score_scale
    )
    grad_keys = (
        jnp.einsum("hqk,qhd->khd", grad_scores, query_heads, preferred_element_type=jnp.float32)
        * score_scale
    )
    pieces_list = [grad_queries, grad_keys, grad_values]
    return jnp.concatenate(
        [p.astype(jnp.bfloat16).reshape(row_count, -1) for p in pieces_list], axis=1
    )


def body(tokens, w_qkv, w_out, doc_blocks, cotangent):
    row_count = tokens.shape[0]
    head_width = w_out.shape[1]
    head_count = H
    all_devices = lax.axis_size("dp") * lax.axis_size("fsdp")
    allowed = row_mask(doc_blocks[0], row_count)
    columns = tokens
    qkv = jnp.dot(
        columns,
        lax.all_gather(w_qkv, "fsdp", axis=0, tiled=True),
        preferred_element_type=jnp.float32,
    ).astype(jnp.bfloat16)
    query_rows = qkv[:, :head_width]
    key_rows = qkv[:, head_width : 2 * head_width]
    value_rows = qkv[:, 2 * head_width :]
    mixed, attn_probs, probs_half = attend_forward(
        query_rows, key_rows, value_rows, allowed, head_count
    )
    output = lax.dot_general(
        mixed,
        lax.all_gather(w_out, "fsdp", axis=0, tiled=True),
        CONTRACT_COLS,
        preferred_element_type=jnp.float32,
    )
    columns = cotangent
    grad_mixed = jnp.dot(
        columns,
        lax.all_gather(w_out, "fsdp", axis=0, tiled=True),
        preferred_element_type=jnp.float32,
    ).astype(jnp.bfloat16)
    output = output.astype(jnp.bfloat16)
    grad_qkv = attend_backward(
        query_rows, key_rows, value_rows, attn_probs, probs_half, grad_mixed, head_count
    )
    grad_tokens = lax.dot_general(
        grad_qkv,
        lax.all_gather(w_qkv, "fsdp", axis=0, tiled=True),
        CONTRACT_COLS,
        preferred_element_type=jnp.float32,
    )
    grad_tokens = grad_tokens.astype(jnp.bfloat16)
    first_term = lax.dot_general(
        tokens, grad_qkv, CONTRACT_ROWS, preferred_element_type=jnp.float32
    )
    second_term = lax.dot_general(
        cotangent, mixed, CONTRACT_ROWS, preferred_element_type=jnp.float32
    )
    partial_grad = lax.psum_scatter(
        jnp.concatenate([first_term, second_term], axis=1), "fsdp", scatter_dimension=0, tiled=True
    )
    summed = lax.psum(partial_grad, "dp")
    norm_factor = 1.0 / math.sqrt(row_count * all_devices)
    grad_w_qkv = summed[:, : 3 * head_width] * norm_factor
    grad_w_out = summed[:, 3 * head_width :] * norm_factor
    return (output, grad_tokens, grad_w_qkv, grad_w_out)


MESH = pl.DeviceIdType.MESH
CHUNKS = 4


class Place:
    def __init__(self, fsdp_size):
        self.d, self.f = lax.axis_index("dp"), lax.axis_index("fsdp")
        self.c = lax.rem(self.d, 2)
        chip = lax.div(self.d, 2)
        self.x, self.y = lax.rem(chip, 2), lax.div(chip, 2)
        self.dx = self.dp_of(self.y, 1 - self.x, self.c)
        self.dy = self.dp_of(1 - self.y, self.x, self.c)
        self.dd = self.dp_of(1 - self.y, 1 - self.x, self.c)
        self.dc = self.dp_of(self.y, self.x, 1 - self.c)
        self.n = fsdp_size

    def dp_of(self, y, x, c):
        return (y * 2 + x) * 2 + c

    def ahead(self, j):
        return lax.rem(self.f + j, self.n)

    def behind(self, j):
        return lax.rem(self.f + self.n - j, self.n)

    def barrier(self):
        sem = pltpu.get_barrier_semaphore()
        targets = [(self.dx, self.f), (self.dy, self.f), (self.dc, self.f)]
        targets += [(self.d, self.ahead(j)) for j in range(1, self.n)]
        for target in targets:
            pl.semaphore_signal(sem, inc=1, device_id=target, device_id_type=MESH)
        pl.semaphore_wait(sem, len(targets))


def remote(src, dst, send_sem, recv_sem, target):
    return pltpu.make_async_remote_copy(
        src_ref=src,
        dst_ref=dst,
        send_sem=send_sem,
        recv_sem=recv_sem,
        device_id=target,
        device_id_type=MESH,
    )


def gather_kernel(n, wq_ref, wo_ref, t_ref, c_ref, fq_ref, fo_ref, tt_ref, ct_ref, send, recv, local_sem):
    me = Place(n)
    rows = wq_ref.shape[0]
    share = rows // 8
    half = share // 2
    mine, whole = (wq_ref, wo_ref), (fq_ref, fo_ref)
    me.barrier()
    started = {}

    def span(a, f, d, first, count):
        start = pl.multiple_of(f * rows + d * share + first, half)
        return whole[a].at[pl.ds(start, count)]

    def push(a, kind, j, f, d, first, count, target):
        spot = span(a, f, d, first, count)
        source = spot
        if kind == 0:
            source = mine[a].at[pl.ds(pl.multiple_of(d * share, share), share)]
        slot = kind * (n - 1) + j - 1
        copy = remote(source, spot, send.at[a, slot], recv.at[a, slot], target)
        copy.start()
        started[a, kind, j] = copy

    for j in range(1, n):
        for a in range(2):
            push(a, 0, j, me.f, me.d, 0, share, (me.d, me.ahead(j)))
    locals_ = []
    for a in range(2):
        start = pl.multiple_of(me.f * rows, rows)
        copy = pltpu.make_async_copy(mine[a], whole[a].at[pl.ds(start, rows)], local_sem.at[a])
        copy.start()
        locals_.append(copy)

    def turn(i, carry):
        part = pl.ds(pl.multiple_of(i * 128, 128), 128)
        tt_ref[part, :] = t_ref[:, part].T
        ct_ref[part, :] = c_ref[:, part].T
        return carry

    lax.fori_loop(0, t_ref.shape[1] // 128, turn, 0)
    for step in range(1, n + 2):
        for a in range(2):
            j = step
            if j < n:
                f = me.behind(j)
                started[a, 0, j].wait_recv()
                push(a, 1, j, f, me.d, 0, share, (me.dx, me.f))
                push(a, 2, j, f, me.d, 0, share, (me.dy, me.f))
                push(a, 5, j, f, me.d, 0, share, (me.dc, me.f))
            j = step - 1
            if 1 <= j < n:
                f = me.behind(j)
                started[a, 1, j].wait_recv()
                push(a, 3, j, f, me.dx, 0, half, (me.dy, me.f))
                push(a, 6, j, f, me.dx, 0, share, (me.dc, me.f))
                started[a, 2, j].wait_recv()
                push(a, 4, j, f, me.dy, half, half, (me.dx, me.f))
                push(a, 7, j, f, me.dy, 0, share, (me.dc, me.f))
            j = step - 2
            if 1 <= j < n:
                f = me.behind(j)
                started[a, 3, j].wait_recv()
                push(a, 8, j, f, me.dd, 0, half, (me.dc, me.f))
                started[a, 4, j].wait_recv()
                push(a, 9, j, f, me.dd, half, half, (me.dc, me.f))
    for (a, kind, j), copy in started.items():
        copy.wait_send()
        if kind >= 5:
            copy.wait_recv()
    for copy in locals_:
        copy.wait()


def gather_weights(n, w_qkv, w_out, tokens, cotangent):
    vmem = pl.BlockSpec(memory_space=pltpu.VMEM)
    return pl.pallas_call(
        functools.partial(gather_kernel, n),
        out_shape=[
            jax.ShapeDtypeStruct((w.shape[0] * n, w.shape[1]), w.dtype) for w in (w_qkv, w_out)
        ]
        + [jax.ShapeDtypeStruct(t.shape[::-1], t.dtype) for t in (tokens, cotangent)],
        in_specs=[vmem] * 4,
        out_specs=[pl.BlockSpec(memory_space=pl.ANY)] * 2 + [vmem] * 2,
        scratch_shapes=[
            pltpu.SemaphoreType.DMA((2, 10 * (n - 1))),
            pltpu.SemaphoreType.DMA((2, 10 * (n - 1))),
            pltpu.SemaphoreType.DMA((2,)),
        ],
        compiler_params=pltpu.CompilerParams(collective_id=0, has_side_effects=True),
        name="gather_weights",
    )(w_qkv, w_out, tokens, cotangent)


def add_half(left, right):
    return left.astype(jnp.float32) + right.astype(jnp.float32)


def reduce_kernel(
    n,
    tt_ref,
    ct_ref,
    grad_ref,
    mixed_ref,
    fq_ref,
    fo_ref,
    sum_ref,
    out_ref,
    grad_tokens_ref,
    wq,
    wo,
    grads,
    core_sum,
    pair_sum,
    plane_sum,
    z_terms,
    send,
    recv,
    local_sem,
):
    me = Place(n)
    width = mixed_ref.shape[-1]
    share = grads.shape[-2]
    half = share // 2
    loads = []
    for i, (src, dst) in enumerate(((fq_ref, wq), (fo_ref, wo))):
        copy = pltpu.make_async_copy(src, dst, local_sem.at[i])
        copy.start()
        loads.append(copy)
    me.barrier()
    started = {}

    def weight_grad(k):
        def rows_of(f, carry):
            rows = pl.ds(pl.multiple_of(f * share * 8, share * 8), share * 8)
            if k == CHUNKS - 1:
                left, right = ct_ref[rows, :], mixed_ref[...]
            else:
                left, right = tt_ref[rows, :], grad_ref[:, k * width : (k + 1) * width]
            part = jnp.dot(left, right, preferred_element_type=jnp.float32)
            grads[k, f] = part.astype(jnp.bfloat16).reshape(2, 2, 2, share, width)
            return carry

        lax.fori_loop(0, n, rows_of, 0)

    def times_weights(left_ref, weight, target_ref):
        def columns_of(i, carry):
            cols = pl.ds(pl.multiple_of(i * 256, 256), 256)
            part = lax.dot_general(
                left_ref[...], weight[cols, :], CONTRACT_COLS, preferred_element_type=jnp.float32
            )
            target_ref[:, cols] = part.astype(jnp.bfloat16)
            return carry

        lax.fori_loop(0, weight.shape[0] // 256, columns_of, 0)

    def push(k, kind, src, dst, target):
        copy = remote(src, dst, send.at[k, kind], recv.at[k, kind], target)
        copy.start()
        started[k, kind] = copy

    def columns(k):
        return pl.ds(k * width, width)

    def core_start(k):
        push(k, 0, grads.at[k, :, :, :, 1 - me.c], core_sum.at[k], (me.dc, me.f))

    def stage_core(k):
        started[k, 0].wait_recv()

        def add(i, carry):
            f, y, x = lax.div(i, 4), lax.rem(lax.div(i, 2), 2), lax.rem(i, 2)
            total = add_half(grads[k, f, y, x, me.c], core_sum[k, f, y, x])
            core_sum[k, f, y, x] = total.astype(jnp.bfloat16)
            return carry

        lax.fori_loop(0, n * 4, add, 0)
        if k % 2 == 0:
            push(k, 1, core_sum.at[k, :, :, 1 - me.x], pair_sum.at[k], (me.dx, me.f))
        else:
            push(k, 1, core_sum.at[k, :, 1 - me.y], pair_sum.at[k], (me.dy, me.f))

    def stage_pair(k):
        started[k, 1].wait_recv()

        def add(i, carry):
            f, other = lax.div(i, 2), lax.rem(i, 2)
            own = core_sum[k, f, other, me.x] if k % 2 == 0 else core_sum[k, f, me.y, other]
            pair_sum[k, f, other] = add_half(own, pair_sum[k, f, other]).astype(jnp.bfloat16)
            return carry

        lax.fori_loop(0, n * 2, add, 0)
        if k % 2 == 0:
            push(k, 2, pair_sum.at[k, :, 1 - me.y], plane_sum.at[k], (me.dy, me.f))
        else:
            push(k, 2, pair_sum.at[k, :, 1 - me.x], plane_sum.at[k], (me.dx, me.f))

    def stage_plane(k):
        started[k, 2].wait_recv()
        keep = me.y if k % 2 == 0 else me.x

        def add(f, carry):
            plane_sum[k, f] = add_half(pair_sum[k, f, keep], plane_sum[k, f]).astype(jnp.bfloat16)
            return carry

        lax.fori_loop(0, n, add, 0)
        for j in range(1, n):
            push(k, 2 + j, plane_sum.at[k, me.ahead(j)], z_terms.at[k, j - 1], (me.d, me.ahead(j)))

    base = 2 + n

    def stage_z(k):
        total = plane_sum[k, me.f].astype(jnp.float32)
        for j in range(1, n):
            started[k, 2 + j].wait_recv()
            total = total + z_terms[k, j - 1].astype(jnp.float32)
        sum_ref[me.d, :, columns(k)] = total.astype(jnp.bfloat16)
        spot = sum_ref.at[me.d, :, columns(k)]
        push(k, base, spot, spot, (me.dx, me.f))
        push(k, base + 1, spot, spot, (me.dy, me.f))
        push(k, base + 4, spot, spot, (me.dc, me.f))

    def stage_spread(k):
        started[k, base].wait_recv()
        spot = sum_ref.at[me.dx, pl.ds(0, half), columns(k)]
        push(k, base + 2, spot, spot, (me.dy, me.f))
        spot = sum_ref.at[me.dx, :, columns(k)]
        push(k, base + 5, spot, spot, (me.dc, me.f))
        started[k, base + 1].wait_recv()
        spot = sum_ref.at[me.dy, pl.ds(half, half), columns(k)]
        push(k, base + 3, spot, spot, (me.dx, me.f))
        spot = sum_ref.at[me.dy, :, columns(k)]
        push(k, base + 6, spot, spot, (me.dc, me.f))

    def stage_last(k):
        started[k, base + 2].wait_recv()
        spot = sum_ref.at[me.dd, pl.ds(0, half), columns(k)]
        push(k, base + 7, spot, spot, (me.dc, me.f))
        started[k, base + 3].wait_recv()
        spot = sum_ref.at[me.dd, pl.ds(half, half), columns(k)]
        push(k, base + 8, spot, spot, (me.dc, me.f))

    order = [CHUNKS - 1] + list(range(CHUNKS - 1))
    weight_grad(order[0])
    for before, k in zip(order, order[1:]):
        weight_grad(k)
        core_start(before)
        if before != order[0]:
            stage_core(order[order.index(before) - 1])
    core_start(order[-1])
    stage_core(order[-2])
    stage_core(order[-1])
    for copy in loads:
        copy.wait()
    times_weights(grad_ref, wq, grad_tokens_ref)
    first, second = order[: CHUNKS // 2], order[CHUNKS // 2 :]
    for k in first:
        stage_pair(k)
    times_weights(mixed_ref, wo, out_ref)
    plan = [
        (stage_plane, first),
        (stage_pair, second),
        (stage_z, first),
        (stage_plane, second),
        (stage_spread, first),
        (stage_z, second),
        (stage_last, first),
        (stage_spread, second),
        (stage_last, second),
    ]
    for stage, group in plan:
        for k in group:
            stage(k)
    for (k, kind), copy in started.items():
        copy.wait_send()
        if kind >= base + 4:
            copy.wait_recv()


def reduce_grads(n, tokens_t, cotangent_t, grad_qkv, mixed, full_qkv, full_out):
    features, rows = tokens_t.shape
    share = features // (n * 8)
    width = mixed.shape[1]
    kinds = 2 + n + 9
    vmem = pl.BlockSpec(memory_space=pltpu.VMEM)
    anywhere = pl.BlockSpec(memory_space=pl.ANY)
    return pl.pallas_call(
        functools.partial(reduce_kernel, n),
        out_shape=[
            jax.ShapeDtypeStruct((8, share, CHUNKS * width), jnp.bfloat16),
            jax.ShapeDtypeStruct((rows, features), jnp.bfloat16),
            jax.ShapeDtypeStruct((rows, features), jnp.bfloat16),
        ],
        in_specs=[vmem] * 4 + [anywhere] * 2,
        out_specs=[vmem] * 3,
        scratch_shapes=[
            pltpu.VMEM(full_qkv.shape, jnp.bfloat16),
            pltpu.VMEM(full_out.shape, jnp.bfloat16),
            pltpu.VMEM((CHUNKS, n, 2, 2, 2, share, width), jnp.bfloat16),
            pltpu.VMEM((CHUNKS, n, 2, 2, share, width), jnp.bfloat16),
            pltpu.VMEM((CHUNKS, n, 2, share, width), jnp.bfloat16),
            pltpu.VMEM((CHUNKS, n, share, width), jnp.bfloat16),
            pltpu.VMEM((CHUNKS, n - 1, share, width), jnp.bfloat16),
            pltpu.SemaphoreType.DMA((CHUNKS, kinds)),
            pltpu.SemaphoreType.DMA((CHUNKS, kinds)),
            pltpu.SemaphoreType.DMA((2,)),
        ],
        compiler_params=pltpu.CompilerParams(
            collective_id=1, has_side_effects=True, vmem_limit_bytes=54 << 20
        ),
        name="reduce_grads",
    )(tokens_t, cotangent_t, grad_qkv, mixed, full_qkv, full_out)


def chip_body(tokens, w_qkv, w_out, doc_blocks, cotangent):
    row_count = tokens.shape[0]
    head_width = w_out.shape[1]
    n = lax.axis_size("fsdp")
    all_devices = lax.axis_size("dp") * n
    allowed = row_mask(doc_blocks[0], row_count)
    full_qkv, full_out, tokens_t, cotangent_t = gather_weights(
        n, w_qkv, w_out, tokens, cotangent
    )
    qkv = jnp.dot(tokens, full_qkv, preferred_element_type=jnp.float32).astype(jnp.bfloat16)
    query_rows = qkv[:, :head_width]
    key_rows = qkv[:, head_width : 2 * head_width]
    value_rows = qkv[:, 2 * head_width :]
    mixed, attn_probs, probs_half = attend_forward(query_rows, key_rows, value_rows, allowed, H)
    grad_mixed = jnp.dot(cotangent, full_out, preferred_element_type=jnp.float32)
    grad_mixed = grad_mixed.astype(jnp.bfloat16)
    grad_qkv = attend_backward(
        query_rows, key_rows, value_rows, attn_probs, probs_half, grad_mixed, H
    )
    summed, output, grad_tokens = reduce_grads(
        n, tokens_t, cotangent_t, grad_qkv, mixed, full_qkv, full_out
    )
    summed = summed.reshape(w_out.shape[0], 4 * head_width).astype(jnp.float32)
    norm_factor = 1.0 / math.sqrt(row_count * all_devices)
    grad_w_qkv = summed[:, : 3 * head_width] * norm_factor
    grad_w_out = summed[:, 3 * head_width :] * norm_factor
    return (output, grad_tokens, grad_w_qkv, grad_w_out)


def solution(mesh):
    placed = (
        P(("dp", "fsdp"), None),
        P("fsdp", None),
        P("fsdp", None),
        P(("dp", "fsdp"), None),
        P(("dp", "fsdp"), None),
    )
    in_plane = mesh.shape["dp"] == 8 and mesh.shape["fsdp"] == 4
    return jax.shard_map(
        chip_body if in_plane else body,
        mesh=mesh,
        in_specs=placed,
        out_specs=(
            P(("dp", "fsdp"), None),
            P(("dp", "fsdp"), None),
            P("fsdp", None),
            P("fsdp", None),
        ),
        check_vma=False,
    )
```

```python
import functools
import math

import jax
import jax.numpy as jnp
from jax import lax
from jax.experimental import pallas as pl
from jax.experimental.pallas import tpu as pltpu
from jax.sharding import PartitionSpec as P

H = 8


NEG_FILL = -1e30
CONTRACT_ROWS = (((0,), (0,)), ((), ()))
CONTRACT_COLS = (((1,), (1,)), ((), ()))


def row_mask(doc_ids, row_count):
    block_len = row_count // doc_ids.shape[0]
    doc_rows = jnp.repeat(doc_ids, block_len, total_repeat_length=row_count)
    position = jnp.arange(row_count, dtype=jnp.int32)
    causal = position[None, :] <= position[:, None]
    return causal & (doc_rows[None, :] == doc_rows[:, None])


def split_heads(matrix, head_count):
    return matrix.reshape(matrix.shape[0], head_count, matrix.shape[1] // head_count)


def attend_forward(query_rows, key_rows, value_rows, allowed, head_count):
    row_count = query_rows.shape[0]
    query_heads = split_heads(query_rows, head_count)
    key_heads = split_heads(key_rows, head_count)
    value_heads = split_heads(value_rows, head_count)
    score_scale = query_heads.shape[2] ** (-0.5)
    scores = (
        jnp.einsum("qhd,khd->hqk", query_heads, key_heads, preferred_element_type=jnp.float32)
        * score_scale
    )
    scores = jnp.where(allowed[None], scores, NEG_FILL)
    highest = jnp.max(scores, axis=-1, keepdims=True)
    expvals = jnp.exp(scores - highest)
    attn_probs = expvals / jnp.sum(expvals, axis=-1, keepdims=True)
    probs_half = attn_probs.astype(jnp.bfloat16)
    mixed = jnp.einsum("hqk,khd->qhd", probs_half, value_heads, preferred_element_type=jnp.float32)
    return (mixed.astype(jnp.bfloat16).reshape(row_count, -1), attn_probs, probs_half)


def attend_backward(
    query_rows, key_rows, value_rows, attn_probs, probs_half, grad_mixed, head_count
):
    row_count = query_rows.shape[0]
    query_heads = split_heads(query_rows, head_count)
    key_heads = split_heads(key_rows, head_count)
    value_heads = split_heads(value_rows, head_count)
    grad_heads = split_heads(grad_mixed, head_count)
    score_scale = query_heads.shape[2] ** (-0.5)
    grad_probs = jnp.einsum(
        "qhd,khd->hqk", grad_heads, value_heads, preferred_element_type=jnp.float32
    )
    grad_values = jnp.einsum(
        "hqk,qhd->khd", probs_half, grad_heads, preferred_element_type=jnp.float32
    )
    inner = jnp.sum(attn_probs * grad_probs, axis=-1, keepdims=True)
    grad_scores = (attn_probs * (grad_probs - inner)).astype(jnp.bfloat16)
    grad_queries = (
        jnp.einsum("hqk,khd->qhd", grad_scores, key_heads, preferred_element_type=jnp.float32)
        * score_scale
    )
    grad_keys = (
        jnp.einsum("hqk,qhd->khd", grad_scores, query_heads, preferred_element_type=jnp.float32)
        * score_scale
    )
    pieces_list = [grad_queries, grad_keys, grad_values]
    return jnp.concatenate(
        [p.astype(jnp.bfloat16).reshape(row_count, -1) for p in pieces_list], axis=1
    )


def body(tokens, w_qkv, w_out, doc_blocks, cotangent):
    row_count = tokens.shape[0]
    head_width = w_out.shape[1]
    head_count = H
    all_devices = lax.axis_size("dp") * lax.axis_size("fsdp")
    allowed = row_mask(doc_blocks[0], row_count)
    columns = tokens
    qkv = jnp.dot(
        columns,
        lax.all_gather(w_qkv, "fsdp", axis=0, tiled=True),
        preferred_element_type=jnp.float32,
    ).astype(jnp.bfloat16)
    query_rows = qkv[:, :head_width]
    key_rows = qkv[:, head_width : 2 * head_width]
    value_rows = qkv[:, 2 * head_width :]
    mixed, attn_probs, probs_half = attend_forward(
        query_rows, key_rows, value_rows, allowed, head_count
    )
    output = lax.dot_general(
        mixed,
        lax.all_gather(w_out, "fsdp", axis=0, tiled=True),
        CONTRACT_COLS,
        preferred_element_type=jnp.float32,
    )
    columns = cotangent
    grad_mixed = jnp.dot(
        columns,
        lax.all_gather(w_out, "fsdp", axis=0, tiled=True),
        preferred_element_type=jnp.float32,
    ).astype(jnp.bfloat16)
    output = output.astype(jnp.bfloat16)
    grad_qkv = attend_backward(
        query_rows, key_rows, value_rows, attn_probs, probs_half, grad_mixed, head_count
    )
    grad_tokens = lax.dot_general(
        grad_qkv,
        lax.all_gather(w_qkv, "fsdp", axis=0, tiled=True),
        CONTRACT_COLS,
        preferred_element_type=jnp.float32,
    )
    grad_tokens = grad_tokens.astype(jnp.bfloat16)
    first_term = lax.dot_general(
        tokens, grad_qkv, CONTRACT_ROWS, preferred_element_type=jnp.float32
    )
    second_term = lax.dot_general(
        cotangent, mixed, CONTRACT_ROWS, preferred_element_type=jnp.float32
    )
    partial_grad = lax.psum_scatter(
        jnp.concatenate([first_term, second_term], axis=1), "fsdp", scatter_dimension=0, tiled=True
    )
    summed = lax.psum(partial_grad, "dp")
    norm_factor = 1.0 / math.sqrt(row_count * all_devices)
    grad_w_qkv = summed[:, : 3 * head_width] * norm_factor
    grad_w_out = summed[:, 3 * head_width :] * norm_factor
    return (output, grad_tokens, grad_w_qkv, grad_w_out)


MESH = pl.DeviceIdType.MESH
CHUNKS = 8


class Place:
    def __init__(self, fsdp_size):
        self.d, self.f = lax.axis_index("dp"), lax.axis_index("fsdp")
        self.c = lax.rem(self.d, 2)
        chip = lax.div(self.d, 2)
        self.x, self.y = lax.rem(chip, 2), lax.div(chip, 2)
        self.dx = self.dp_of(self.y, 1 - self.x, self.c)
        self.dy = self.dp_of(1 - self.y, self.x, self.c)
        self.dd = self.dp_of(1 - self.y, 1 - self.x, self.c)
        self.dc = self.dp_of(self.y, self.x, 1 - self.c)
        self.n = fsdp_size

    def dp_of(self, y, x, c):
        return (y * 2 + x) * 2 + c

    def ahead(self, j):
        return lax.rem(self.f + j, self.n)

    def behind(self, j):
        return lax.rem(self.f + self.n - j, self.n)

    def barrier(self):
        sem = pltpu.get_barrier_semaphore()
        targets = [(self.dx, self.f), (self.dy, self.f), (self.dc, self.f)]
        targets += [(self.d, self.ahead(j)) for j in range(1, self.n)]
        for target in targets:
            pl.semaphore_signal(sem, inc=1, device_id=target, device_id_type=MESH)
        pl.semaphore_wait(sem, len(targets))


def remote(src, dst, send_sem, recv_sem, target):
    return pltpu.make_async_remote_copy(
        src_ref=src,
        dst_ref=dst,
        send_sem=send_sem,
        recv_sem=recv_sem,
        device_id=target,
        device_id_type=MESH,
    )


def gather_kernel(n, wq_ref, wo_ref, t_ref, c_ref, fq_ref, fo_ref, tt_ref, ct_ref, send, recv, local_sem):
    me = Place(n)
    rows = wq_ref.shape[0]
    share = rows // 8
    half = share // 2
    mine, whole = (wq_ref, wo_ref), (fq_ref, fo_ref)
    me.barrier()
    started = {}

    def span(a, f, d, first, count):
        start = pl.multiple_of(f * rows + d * share + first, half)
        return whole[a].at[pl.ds(start, count)]

    def push(a, kind, j, f, d, first, count, target):
        spot = span(a, f, d, first, count)
        source = spot
        if kind == 0:
            source = mine[a].at[pl.ds(pl.multiple_of(d * share, share), share)]
        slot = kind * (n - 1) + j - 1
        copy = remote(source, spot, send.at[a, slot], recv.at[a, slot], target)
        copy.start()
        started[a, kind, j] = copy

    for j in range(1, n):
        for a in range(2):
            push(a, 0, j, me.f, me.d, 0, share, (me.d, me.ahead(j)))
    locals_ = []
    for a in range(2):
        start = pl.multiple_of(me.f * rows, rows)
        copy = pltpu.make_async_copy(mine[a], whole[a].at[pl.ds(start, rows)], local_sem.at[a])
        copy.start()
        locals_.append(copy)

    def turn(i, carry):
        part = pl.ds(pl.multiple_of(i * 128, 128), 128)
        tt_ref[part, :] = t_ref[:, part].T
        ct_ref[part, :] = c_ref[:, part].T
        return carry

    lax.fori_loop(0, t_ref.shape[1] // 128, turn, 0)
    for step in range(1, n + 2):
        for a in range(2):
            j = step
            if j < n:
                f = me.behind(j)
                started[a, 0, j].wait_recv()
                push(a, 1, j, f, me.d, 0, share, (me.dx, me.f))
                push(a, 2, j, f, me.d, 0, share, (me.dy, me.f))
                push(a, 5, j, f, me.d, 0, share, (me.dc, me.f))
            j = step - 1
            if 1 <= j < n:
                f = me.behind(j)
                started[a, 1, j].wait_recv()
                push(a, 3, j, f, me.dx, 0, half, (me.dy, me.f))
                push(a, 6, j, f, me.dx, 0, share, (me.dc, me.f))
                started[a, 2, j].wait_recv()
                push(a, 4, j, f, me.dy, half, half, (me.dx, me.f))
                push(a, 7, j, f, me.dy, 0, share, (me.dc, me.f))
            j = step - 2
            if 1 <= j < n:
                f = me.behind(j)
                started[a, 3, j].wait_recv()
                push(a, 8, j, f, me.dd, 0, half, (me.dc, me.f))
                started[a, 4, j].wait_recv()
                push(a, 9, j, f, me.dd, half, half, (me.dc, me.f))
    for (a, kind, j), copy in started.items():
        copy.wait_send()
        if kind >= 5:
            copy.wait_recv()
    for copy in locals_:
        copy.wait()


def gather_weights(n, w_qkv, w_out, tokens, cotangent):
    vmem = pl.BlockSpec(memory_space=pltpu.VMEM)
    return pl.pallas_call(
        functools.partial(gather_kernel, n),
        out_shape=[
            jax.ShapeDtypeStruct((w.shape[0] * n, w.shape[1]), w.dtype) for w in (w_qkv, w_out)
        ]
        + [jax.ShapeDtypeStruct(t.shape[::-1], t.dtype) for t in (tokens, cotangent)],
        in_specs=[vmem] * 4,
        out_specs=[pl.BlockSpec(memory_space=pl.ANY)] * 2 + [vmem] * 2,
        scratch_shapes=[
            pltpu.SemaphoreType.DMA((2, 10 * (n - 1))),
            pltpu.SemaphoreType.DMA((2, 10 * (n - 1))),
            pltpu.SemaphoreType.DMA((2,)),
        ],
        compiler_params=pltpu.CompilerParams(collective_id=0, has_side_effects=True),
        name="gather_weights",
    )(w_qkv, w_out, tokens, cotangent)


def add_half(left, right):
    return left.astype(jnp.float32) + right.astype(jnp.float32)


def reduce_kernel(
    n,
    tt_ref,
    ct_ref,
    grad_ref,
    mixed_ref,
    fq_ref,
    fo_ref,
    sum_ref,
    out_ref,
    grad_tokens_ref,
    wq,
    wo,
    grads,
    core_sum,
    pair_sum,
    plane_sum,
    z_terms,
    send,
    recv,
    local_sem,
):
    me = Place(n)
    width = 4 * mixed_ref.shape[-1] // CHUNKS
    share = grads.shape[-2]
    half = share // 2
    loads = []
    for i, (src, dst) in enumerate(((fq_ref, wq), (fo_ref, wo))):
        copy = pltpu.make_async_copy(src, dst, local_sem.at[i])
        copy.start()
        loads.append(copy)
    me.barrier()
    started = {}

    def weight_grad(k):
        def rows_of(f, carry):
            rows = pl.ds(pl.multiple_of(f * share * 8, share * 8), share * 8)
            first = k * width
            if first >= grad_ref.shape[1]:
                first -= grad_ref.shape[1]
                left, right = ct_ref[rows, :], mixed_ref[:, first : first + width]
            else:
                left, right = tt_ref[rows, :], grad_ref[:, first : first + width]
            part = jnp.dot(left, right, preferred_element_type=jnp.float32)
            grads[k, f] = part.astype(jnp.bfloat16).reshape(2, 2, 2, share, width)
            return carry

        lax.fori_loop(0, n, rows_of, 0)

    def times_weights(left_ref, weight, target_ref, i):
        cols = pl.ds(i * 256, 256)
        part = lax.dot_general(
            left_ref[...], weight[cols, :], CONTRACT_COLS, preferred_element_type=jnp.float32
        )
        target_ref[:, cols] = part.astype(jnp.bfloat16)

    def push(k, kind, src, dst, target):
        copy = remote(src, dst, send.at[k, kind], recv.at[k, kind], target)
        copy.start()
        started[k, kind] = copy

    def columns(k):
        return pl.ds(k * width, width)

    def core_start(k):
        push(k, 0, grads.at[k, :, :, :, 1 - me.c], core_sum.at[k], (me.dc, me.f))

    def stage_core(k):
        started[k, 0].wait_recv()

        def add(i, carry):
            f, y, x = lax.div(i, 4), lax.rem(lax.div(i, 2), 2), lax.rem(i, 2)
            total = add_half(grads[k, f, y, x, me.c], core_sum[k, f, y, x])
            core_sum[k, f, y, x] = total.astype(jnp.bfloat16)
            return carry

        lax.fori_loop(0, n * 4, add, 0)
        if k % 2 == 0:
            push(k, 1, core_sum.at[k, :, :, 1 - me.x], pair_sum.at[k], (me.dx, me.f))
        else:
            push(k, 1, core_sum.at[k, :, 1 - me.y], pair_sum.at[k], (me.dy, me.f))

    def stage_pair(k):
        started[k, 1].wait_recv()

        def add(i, carry):
            f, other = lax.div(i, 2), lax.rem(i, 2)
            own = core_sum[k, f, other, me.x] if k % 2 == 0 else core_sum[k, f, me.y, other]
            pair_sum[k, f, other] = add_half(own, pair_sum[k, f, other]).astype(jnp.bfloat16)
            return carry

        lax.fori_loop(0, n * 2, add, 0)
        if k % 2 == 0:
            push(k, 2, pair_sum.at[k, :, 1 - me.y], plane_sum.at[k], (me.dy, me.f))
        else:
            push(k, 2, pair_sum.at[k, :, 1 - me.x], plane_sum.at[k], (me.dx, me.f))

    def stage_plane(k):
        started[k, 2].wait_recv()
        keep = me.y if k % 2 == 0 else me.x

        def add(f, carry):
            plane_sum[k, f] = add_half(pair_sum[k, f, keep], plane_sum[k, f]).astype(jnp.bfloat16)
            return carry

        lax.fori_loop(0, n, add, 0)
        for j in range(1, n):
            push(k, 2 + j, plane_sum.at[k, me.ahead(j)], z_terms.at[k, j - 1], (me.d, me.ahead(j)))

    base = 2 + n

    def stage_z(k):
        total = plane_sum[k, me.f].astype(jnp.float32)
        for j in range(1, n):
            started[k, 2 + j].wait_recv()
            total = total + z_terms[k, j - 1].astype(jnp.float32)
        sum_ref[me.d, :, columns(k)] = total.astype(jnp.bfloat16)
        spot = sum_ref.at[me.d, :, columns(k)]
        push(k, base, spot, spot, (me.dx, me.f))
        push(k, base + 1, spot, spot, (me.dy, me.f))
        push(k, base + 4, spot, spot, (me.dc, me.f))

    def stage_spread(k):
        started[k, base].wait_recv()
        spot = sum_ref.at[me.dx, pl.ds(0, half), columns(k)]
        push(k, base + 2, spot, spot, (me.dy, me.f))
        spot = sum_ref.at[me.dx, :, columns(k)]
        push(k, base + 5, spot, spot, (me.dc, me.f))
        started[k, base + 1].wait_recv()
        spot = sum_ref.at[me.dy, pl.ds(half, half), columns(k)]
        push(k, base + 3, spot, spot, (me.dx, me.f))
        spot = sum_ref.at[me.dy, :, columns(k)]
        push(k, base + 6, spot, spot, (me.dc, me.f))

    def stage_last(k):
        started[k, base + 2].wait_recv()
        spot = sum_ref.at[me.dd, pl.ds(0, half), columns(k)]
        push(k, base + 7, spot, spot, (me.dc, me.f))
        started[k, base + 3].wait_recv()
        spot = sum_ref.at[me.dd, pl.ds(half, half), columns(k)]
        push(k, base + 8, spot, spot, (me.dc, me.f))

    order = [CHUNKS - 1, CHUNKS - 2] + list(range(CHUNKS - 2))
    stages = (
        (0, weight_grad),
        (1, core_start),
        (2, stage_core),
        (4, stage_pair),
        (6, stage_plane),
        (8, stage_z),
        (9, stage_spread),
        (10, stage_last),
    )
    pieces = [(grad_ref, wq, grad_tokens_ref, i) for i in range(wq.shape[0] // 256)]
    pieces += [(mixed_ref, wo, out_ref, i) for i in range(wo.shape[0] // 256)]
    for step in range(CHUNKS + 10):
        for after, stage in stages:
            if 0 <= step - after < CHUNKS:
                stage(order[step - after])
        if step == 2:
            for copy in loads:
                copy.wait()
        if step >= 2 and pieces:
            times_weights(*pieces.pop(0))
    for piece in pieces:
        times_weights(*piece)
    for (k, kind), copy in started.items():
        copy.wait_send()
        if kind >= base + 4:
            copy.wait_recv()


def reduce_grads(n, tokens_t, cotangent_t, grad_qkv, mixed, full_qkv, full_out):
    features, rows = tokens_t.shape
    share = features // (n * 8)
    width = 4 * mixed.shape[1] // CHUNKS
    kinds = 2 + n + 9
    vmem = pl.BlockSpec(memory_space=pltpu.VMEM)
    anywhere = pl.BlockSpec(memory_space=pl.ANY)
    return pl.pallas_call(
        functools.partial(reduce_kernel, n),
        out_shape=[
            jax.ShapeDtypeStruct((8, share, CHUNKS * width), jnp.bfloat16),
            jax.ShapeDtypeStruct((rows, features), jnp.bfloat16),
            jax.ShapeDtypeStruct((rows, features), jnp.bfloat16),
        ],
        in_specs=[vmem] * 4 + [anywhere] * 2,
        out_specs=[vmem] * 3,
        scratch_shapes=[
            pltpu.VMEM(full_qkv.shape, jnp.bfloat16),
            pltpu.VMEM(full_out.shape, jnp.bfloat16),
            pltpu.VMEM((CHUNKS, n, 2, 2, 2, share, width), jnp.bfloat16),
            pltpu.VMEM((CHUNKS, n, 2, 2, share, width), jnp.bfloat16),
            pltpu.VMEM((CHUNKS, n, 2, share, width), jnp.bfloat16),
            pltpu.VMEM((CHUNKS, n, share, width), jnp.bfloat16),
            pltpu.VMEM((CHUNKS, n - 1, share, width), jnp.bfloat16),
            pltpu.SemaphoreType.DMA((CHUNKS, kinds)),
            pltpu.SemaphoreType.DMA((CHUNKS, kinds)),
            pltpu.SemaphoreType.DMA((2,)),
        ],
        compiler_params=pltpu.CompilerParams(
            collective_id=1, has_side_effects=True, vmem_limit_bytes=54 << 20
        ),
        name="reduce_grads",
    )(tokens_t, cotangent_t, grad_qkv, mixed, full_qkv, full_out)


def chip_body(tokens, w_qkv, w_out, doc_blocks, cotangent):
    row_count = tokens.shape[0]
    head_width = w_out.shape[1]
    n = lax.axis_size("fsdp")
    all_devices = lax.axis_size("dp") * n
    allowed = row_mask(doc_blocks[0], row_count)
    full_qkv, full_out, tokens_t, cotangent_t = gather_weights(
        n, w_qkv, w_out, tokens, cotangent
    )
    qkv = jnp.dot(tokens, full_qkv, preferred_element_type=jnp.float32).astype(jnp.bfloat16)
    query_rows = qkv[:, :head_width]
    key_rows = qkv[:, head_width : 2 * head_width]
    value_rows = qkv[:, 2 * head_width :]
    mixed, attn_probs, probs_half = attend_forward(query_rows, key_rows, value_rows, allowed, H)
    grad_mixed = jnp.dot(cotangent, full_out, preferred_element_type=jnp.float32)
    grad_mixed = grad_mixed.astype(jnp.bfloat16)
    grad_qkv = attend_backward(
        query_rows, key_rows, value_rows, attn_probs, probs_half, grad_mixed, H
    )
    summed, output, grad_tokens = reduce_grads(
        n, tokens_t, cotangent_t, grad_qkv, mixed, full_qkv, full_out
    )
    summed = summed.reshape(w_out.shape[0], 4 * head_width).astype(jnp.float32)
    norm_factor = 1.0 / math.sqrt(row_count * all_devices)
    grad_w_qkv = summed[:, : 3 * head_width] * norm_factor
    grad_w_out = summed[:, 3 * head_width :] * norm_factor
    return (output, grad_tokens, grad_w_qkv, grad_w_out)


def solution(mesh):
    placed = (
        P(("dp", "fsdp"), None),
        P("fsdp", None),
        P("fsdp", None),
        P(("dp", "fsdp"), None),
        P(("dp", "fsdp"), None),
    )
    in_plane = mesh.shape["dp"] == 8 and mesh.shape["fsdp"] == 4
    return jax.shard_map(
        chip_body if in_plane else body,
        mesh=mesh,
        in_specs=placed,
        out_specs=(
            P(("dp", "fsdp"), None),
            P(("dp", "fsdp"), None),
            P("fsdp", None),
            P("fsdp", None),
        ),
        check_vma=False,
    )
```

```python
import functools
import math

import jax
import jax.numpy as jnp
from jax import lax
from jax.experimental import pallas as pl
from jax.experimental.pallas import tpu as pltpu
from jax.sharding import PartitionSpec as P

H = 8


NEG_FILL = -1e30
CONTRACT_ROWS = (((0,), (0,)), ((), ()))
CONTRACT_COLS = (((1,), (1,)), ((), ()))


def row_mask(doc_ids, row_count):
    block_len = row_count // doc_ids.shape[0]
    doc_rows = jnp.repeat(doc_ids, block_len, total_repeat_length=row_count)
    position = jnp.arange(row_count, dtype=jnp.int32)
    causal = position[None, :] <= position[:, None]
    return causal & (doc_rows[None, :] == doc_rows[:, None])


def split_heads(matrix, head_count):
    return matrix.reshape(matrix.shape[0], head_count, matrix.shape[1] // head_count)


def attend_forward(query_rows, key_rows, value_rows, allowed, head_count):
    row_count = query_rows.shape[0]
    query_heads = split_heads(query_rows, head_count)
    key_heads = split_heads(key_rows, head_count)
    value_heads = split_heads(value_rows, head_count)
    score_scale = query_heads.shape[2] ** (-0.5)
    scores = (
        jnp.einsum("qhd,khd->hqk", query_heads, key_heads, preferred_element_type=jnp.float32)
        * score_scale
    )
    scores = jnp.where(allowed[None], scores, NEG_FILL)
    highest = jnp.max(scores, axis=-1, keepdims=True)
    expvals = jnp.exp(scores - highest)
    attn_probs = expvals / jnp.sum(expvals, axis=-1, keepdims=True)
    probs_half = attn_probs.astype(jnp.bfloat16)
    mixed = jnp.einsum("hqk,khd->qhd", probs_half, value_heads, preferred_element_type=jnp.float32)
    return (mixed.astype(jnp.bfloat16).reshape(row_count, -1), attn_probs, probs_half)


def attend_backward(
    query_rows, key_rows, value_rows, attn_probs, probs_half, grad_mixed, head_count
):
    row_count = query_rows.shape[0]
    query_heads = split_heads(query_rows, head_count)
    key_heads = split_heads(key_rows, head_count)
    value_heads = split_heads(value_rows, head_count)
    grad_heads = split_heads(grad_mixed, head_count)
    score_scale = query_heads.shape[2] ** (-0.5)
    grad_probs = jnp.einsum(
        "qhd,khd->hqk", grad_heads, value_heads, preferred_element_type=jnp.float32
    )
    grad_values = jnp.einsum(
        "hqk,qhd->khd", probs_half, grad_heads, preferred_element_type=jnp.float32
    )
    inner = jnp.sum(attn_probs * grad_probs, axis=-1, keepdims=True)
    grad_scores = (attn_probs * (grad_probs - inner)).astype(jnp.bfloat16)
    grad_queries = (
        jnp.einsum("hqk,khd->qhd", grad_scores, key_heads, preferred_element_type=jnp.float32)
        * score_scale
    )
    grad_keys = (
        jnp.einsum("hqk,qhd->khd", grad_scores, query_heads, preferred_element_type=jnp.float32)
        * score_scale
    )
    pieces_list = [grad_queries, grad_keys, grad_values]
    return jnp.concatenate(
        [p.astype(jnp.bfloat16).reshape(row_count, -1) for p in pieces_list], axis=1
    )


def body(tokens, w_qkv, w_out, doc_blocks, cotangent):
    row_count = tokens.shape[0]
    head_width = w_out.shape[1]
    head_count = H
    all_devices = lax.axis_size("dp") * lax.axis_size("fsdp")
    allowed = row_mask(doc_blocks[0], row_count)
    columns = tokens
    qkv = jnp.dot(
        columns,
        lax.all_gather(w_qkv, "fsdp", axis=0, tiled=True),
        preferred_element_type=jnp.float32,
    ).astype(jnp.bfloat16)
    query_rows = qkv[:, :head_width]
    key_rows = qkv[:, head_width : 2 * head_width]
    value_rows = qkv[:, 2 * head_width :]
    mixed, attn_probs, probs_half = attend_forward(
        query_rows, key_rows, value_rows, allowed, head_count
    )
    output = lax.dot_general(
        mixed,
        lax.all_gather(w_out, "fsdp", axis=0, tiled=True),
        CONTRACT_COLS,
        preferred_element_type=jnp.float32,
    )
    columns = cotangent
    grad_mixed = jnp.dot(
        columns,
        lax.all_gather(w_out, "fsdp", axis=0, tiled=True),
        preferred_element_type=jnp.float32,
    ).astype(jnp.bfloat16)
    output = output.astype(jnp.bfloat16)
    grad_qkv = attend_backward(
        query_rows, key_rows, value_rows, attn_probs, probs_half, grad_mixed, head_count
    )
    grad_tokens = lax.dot_general(
        grad_qkv,
        lax.all_gather(w_qkv, "fsdp", axis=0, tiled=True),
        CONTRACT_COLS,
        preferred_element_type=jnp.float32,
    )
    grad_tokens = grad_tokens.astype(jnp.bfloat16)
    first_term = lax.dot_general(
        tokens, grad_qkv, CONTRACT_ROWS, preferred_element_type=jnp.float32
    )
    second_term = lax.dot_general(
        cotangent, mixed, CONTRACT_ROWS, preferred_element_type=jnp.float32
    )
    partial_grad = lax.psum_scatter(
        jnp.concatenate([first_term, second_term], axis=1), "fsdp", scatter_dimension=0, tiled=True
    )
    summed = lax.psum(partial_grad, "dp")
    norm_factor = 1.0 / math.sqrt(row_count * all_devices)
    grad_w_qkv = summed[:, : 3 * head_width] * norm_factor
    grad_w_out = summed[:, 3 * head_width :] * norm_factor
    return (output, grad_tokens, grad_w_qkv, grad_w_out)


MESH = pl.DeviceIdType.MESH
CHUNKS = 8


class Place:
    def __init__(self, fsdp_size):
        self.d, self.f = lax.axis_index("dp"), lax.axis_index("fsdp")
        self.c = lax.rem(self.d, 2)
        chip = lax.div(self.d, 2)
        self.x, self.y = lax.rem(chip, 2), lax.div(chip, 2)
        self.dx = self.dp_of(self.y, 1 - self.x, self.c)
        self.dy = self.dp_of(1 - self.y, self.x, self.c)
        self.dd = self.dp_of(1 - self.y, 1 - self.x, self.c)
        self.dc = self.dp_of(self.y, self.x, 1 - self.c)
        self.n = fsdp_size

    def dp_of(self, y, x, c):
        return (y * 2 + x) * 2 + c

    def ahead(self, j):
        return lax.rem(self.f + j, self.n)

    def behind(self, j):
        return lax.rem(self.f + self.n - j, self.n)

    def barrier(self):
        sem = pltpu.get_barrier_semaphore()
        targets = [(self.dx, self.f), (self.dy, self.f), (self.dc, self.f)]
        targets += [(self.d, self.ahead(j)) for j in range(1, self.n)]
        for target in targets:
            pl.semaphore_signal(sem, inc=1, device_id=target, device_id_type=MESH)
        pl.semaphore_wait(sem, len(targets))


def remote(src, dst, send_sem, recv_sem, target):
    return pltpu.make_async_remote_copy(
        src_ref=src,
        dst_ref=dst,
        send_sem=send_sem,
        recv_sem=recv_sem,
        device_id=target,
        device_id_type=MESH,
    )


def gather_kernel(n, wq_ref, wo_ref, t_ref, c_ref, fq_ref, fo_ref, tt_ref, ct_ref, send, recv, local_sem):
    me = Place(n)
    rows = wq_ref.shape[0]
    share = rows // 8
    half = share // 2
    mine, whole = (wq_ref, wo_ref), (fq_ref, fo_ref)
    me.barrier()
    started = {}

    def span(a, f, d, first, count):
        start = pl.multiple_of(f * rows + d * share + first, half)
        return whole[a].at[pl.ds(start, count)]

    def push(a, kind, j, f, d, first, count, target):
        spot = span(a, f, d, first, count)
        source = spot
        if kind == 0:
            source = mine[a].at[pl.ds(pl.multiple_of(d * share, share), share)]
        slot = kind * (n - 1) + j - 1
        copy = remote(source, spot, send.at[a, slot], recv.at[a, slot], target)
        copy.start()
        started[a, kind, j] = copy

    for j in range(1, n):
        for a in range(2):
            push(a, 0, j, me.f, me.d, 0, share, (me.d, me.ahead(j)))
    locals_ = []
    for a in range(2):
        start = pl.multiple_of(me.f * rows, rows)
        copy = pltpu.make_async_copy(mine[a], whole[a].at[pl.ds(start, rows)], local_sem.at[a])
        copy.start()
        locals_.append(copy)

    def turn(i, carry):
        part = pl.ds(pl.multiple_of(i * 128, 128), 128)
        tt_ref[part, :] = t_ref[:, part].T
        ct_ref[part, :] = c_ref[:, part].T
        return carry

    lax.fori_loop(0, t_ref.shape[1] // 128, turn, 0)
    for step in range(1, n + 2):
        for a in range(2):
            j = step
            if j < n:
                f = me.behind(j)
                started[a, 0, j].wait_recv()
                push(a, 1, j, f, me.d, 0, share, (me.dx, me.f))
                push(a, 2, j, f, me.d, 0, share, (me.dy, me.f))
                push(a, 5, j, f, me.d, 0, share, (me.dc, me.f))
            j = step - 1
            if 1 <= j < n:
                f = me.behind(j)
                started[a, 1, j].wait_recv()
                push(a, 3, j, f, me.dx, 0, half, (me.dy, me.f))
                push(a, 6, j, f, me.dx, 0, share, (me.dc, me.f))
                started[a, 2, j].wait_recv()
                push(a, 4, j, f, me.dy, half, half, (me.dx, me.f))
                push(a, 7, j, f, me.dy, 0, share, (me.dc, me.f))
            j = step - 2
            if 1 <= j < n:
                f = me.behind(j)
                started[a, 3, j].wait_recv()
                push(a, 8, j, f, me.dd, 0, half, (me.dc, me.f))
                started[a, 4, j].wait_recv()
                push(a, 9, j, f, me.dd, half, half, (me.dc, me.f))
    for (a, kind, j), copy in started.items():
        copy.wait_send()
        if kind >= 5:
            copy.wait_recv()
    for copy in locals_:
        copy.wait()


def gather_weights(n, w_qkv, w_out, tokens, cotangent):
    vmem = pl.BlockSpec(memory_space=pltpu.VMEM)
    return pl.pallas_call(
        functools.partial(gather_kernel, n),
        out_shape=[
            jax.ShapeDtypeStruct((w.shape[0] * n, w.shape[1]), w.dtype) for w in (w_qkv, w_out)
        ]
        + [jax.ShapeDtypeStruct(t.shape[::-1], t.dtype) for t in (tokens, cotangent)],
        in_specs=[vmem] * 4,
        out_specs=[pl.BlockSpec(memory_space=pl.ANY)] * 2 + [vmem] * 2,
        scratch_shapes=[
            pltpu.SemaphoreType.DMA((2, 10 * (n - 1))),
            pltpu.SemaphoreType.DMA((2, 10 * (n - 1))),
            pltpu.SemaphoreType.DMA((2,)),
        ],
        compiler_params=pltpu.CompilerParams(collective_id=0, has_side_effects=True),
        name="gather_weights",
    )(w_qkv, w_out, tokens, cotangent)


def add_half(left, right):
    return left.astype(jnp.float32) + right.astype(jnp.float32)


def reduce_kernel(
    n,
    tt_ref,
    ct_ref,
    grad_ref,
    mixed_ref,
    fq_ref,
    fo_ref,
    sum_ref,
    out_ref,
    grad_tokens_ref,
    wq,
    wo,
    grads,
    core_sum,
    pair_sum,
    plane_sum,
    z_terms,
    send,
    recv,
    local_sem,
):
    me = Place(n)
    width = 4 * mixed_ref.shape[-1] // CHUNKS
    share = grads.shape[-2]
    half = share // 2
    loads = []
    for i, (src, dst) in enumerate(((fq_ref, wq), (fo_ref, wo))):
        copy = pltpu.make_async_copy(src, dst, local_sem.at[i])
        copy.start()
        loads.append(copy)
    me.barrier()
    started = {}

    def weight_grad(k):
        def rows_of(f, carry):
            rows = pl.ds(pl.multiple_of(f * share * 8, share * 8), share * 8)
            first = k * width
            part, first = divmod(first, mixed_ref.shape[1])
            if part == 3:
                left, right = ct_ref[rows, :], mixed_ref[:, first : first + width]
            else:
                left, right = tt_ref[rows, :], grad_ref[part, :, first : first + width]
            part = jnp.dot(left, right, preferred_element_type=jnp.float32)
            grads[k, f] = part.astype(jnp.bfloat16).reshape(2, 2, 2, share, width)
            return carry

        lax.fori_loop(0, n, rows_of, 0)

    def times_weights(lefts, weight, target_ref, i):
        cols = pl.ds(i * 256, 256)
        total = None
        for p, left_ref in enumerate(lefts):
            deep = left_ref.shape[1]
            right = weight[cols, p * deep : (p + 1) * deep]
            part = lax.dot_general(
                left_ref[...], right, CONTRACT_COLS, preferred_element_type=jnp.float32
            )
            total = part if total is None else total + part
        target_ref[:, cols] = total.astype(jnp.bfloat16)

    def push(k, kind, src, dst, target):
        copy = remote(src, dst, send.at[k, kind], recv.at[k, kind], target)
        copy.start()
        started[k, kind] = copy

    def columns(k):
        return pl.ds(k * width, width)

    def core_start(k):
        push(k, 0, grads.at[k, :, :, :, 1 - me.c], core_sum.at[k], (me.dc, me.f))

    def stage_core(k):
        started[k, 0].wait_recv()

        def add(i, carry):
            f, y, x = lax.div(i, 4), lax.rem(lax.div(i, 2), 2), lax.rem(i, 2)
            total = add_half(grads[k, f, y, x, me.c], core_sum[k, f, y, x])
            core_sum[k, f, y, x] = total.astype(jnp.bfloat16)
            return carry

        lax.fori_loop(0, n * 4, add, 0)
        if k % 2 == 0:
            push(k, 1, core_sum.at[k, :, :, 1 - me.x], pair_sum.at[k], (me.dx, me.f))
        else:
            push(k, 1, core_sum.at[k, :, 1 - me.y], pair_sum.at[k], (me.dy, me.f))

    def stage_pair(k):
        started[k, 1].wait_recv()

        def add(i, carry):
            f, other = lax.div(i, 2), lax.rem(i, 2)
            own = core_sum[k, f, other, me.x] if k % 2 == 0 else core_sum[k, f, me.y, other]
            pair_sum[k, f, other] = add_half(own, pair_sum[k, f, other]).astype(jnp.bfloat16)
            return carry

        lax.fori_loop(0, n * 2, add, 0)
        if k % 2 == 0:
            push(k, 2, pair_sum.at[k, :, 1 - me.y], plane_sum.at[k], (me.dy, me.f))
        else:
            push(k, 2, pair_sum.at[k, :, 1 - me.x], plane_sum.at[k], (me.dx, me.f))

    def stage_plane(k):
        started[k, 2].wait_recv()
        keep = me.y if k % 2 == 0 else me.x

        def add(f, carry):
            plane_sum[k, f] = add_half(pair_sum[k, f, keep], plane_sum[k, f]).astype(jnp.bfloat16)
            return carry

        lax.fori_loop(0, n, add, 0)
        for j in range(1, n):
            push(k, 2 + j, plane_sum.at[k, me.ahead(j)], z_terms.at[k, j - 1], (me.d, me.ahead(j)))

    base = 2 + n

    def stage_z(k):
        total = plane_sum[k, me.f].astype(jnp.float32)
        for j in range(1, n):
            started[k, 2 + j].wait_recv()
            total = total + z_terms[k, j - 1].astype(jnp.float32)
        sum_ref[me.d, :, columns(k)] = total.astype(jnp.bfloat16)
        spot = sum_ref.at[me.d, :, columns(k)]
        push(k, base, spot, spot, (me.dx, me.f))
        push(k, base + 1, spot, spot, (me.dy, me.f))
        push(k, base + 4, spot, spot, (me.dc, me.f))

    def stage_spread(k):
        started[k, base].wait_recv()
        spot = sum_ref.at[me.dx, pl.ds(0, half), columns(k)]
        push(k, base + 2, spot, spot, (me.dy, me.f))
        spot = sum_ref.at[me.dx, :, columns(k)]
        push(k, base + 5, spot, spot, (me.dc, me.f))
        started[k, base + 1].wait_recv()
        spot = sum_ref.at[me.dy, pl.ds(half, half), columns(k)]
        push(k, base + 3, spot, spot, (me.dx, me.f))
        spot = sum_ref.at[me.dy, :, columns(k)]
        push(k, base + 6, spot, spot, (me.dc, me.f))

    def stage_last(k):
        started[k, base + 2].wait_recv()
        spot = sum_ref.at[me.dd, pl.ds(0, half), columns(k)]
        push(k, base + 7, spot, spot, (me.dc, me.f))
        started[k, base + 3].wait_recv()
        spot = sum_ref.at[me.dd, pl.ds(half, half), columns(k)]
        push(k, base + 8, spot, spot, (me.dc, me.f))

    order = [CHUNKS - 1, CHUNKS - 2] + list(range(CHUNKS - 2))
    stages = (
        (0, weight_grad),
        (1, core_start),
        (2, stage_core),
        (4, stage_pair),
        (6, stage_plane),
        (8, stage_z),
        (9, stage_spread),
        (10, stage_last),
    )
    lefts = [grad_ref.at[p] for p in range(3)]
    pieces = [(lefts, wq, grad_tokens_ref, i) for i in range(wq.shape[0] // 256)]
    pieces += [([mixed_ref], wo, out_ref, i) for i in range(wo.shape[0] // 256)]
    for step in range(CHUNKS + 10):
        for after, stage in stages:
            if 0 <= step - after < CHUNKS:
                stage(order[step - after])
        if step == 2:
            for copy in loads:
                copy.wait()
        if step >= 2 and pieces:
            times_weights(*pieces.pop(0))
    for piece in pieces:
        times_weights(*piece)
    for (k, kind), copy in started.items():
        copy.wait_send()
        if kind >= base + 4:
            copy.wait_recv()


def reduce_grads(n, tokens_t, cotangent_t, grad_qkv, mixed, full_qkv, full_out):
    features, rows = tokens_t.shape
    share = features // (n * 8)
    width = 4 * mixed.shape[1] // CHUNKS
    kinds = 2 + n + 9
    vmem = pl.BlockSpec(memory_space=pltpu.VMEM)
    anywhere = pl.BlockSpec(memory_space=pl.ANY)
    return pl.pallas_call(
        functools.partial(reduce_kernel, n),
        out_shape=[
            jax.ShapeDtypeStruct((8, share, CHUNKS * width), jnp.bfloat16),
            jax.ShapeDtypeStruct((rows, features), jnp.bfloat16),
            jax.ShapeDtypeStruct((rows, features), jnp.bfloat16),
        ],
        in_specs=[vmem] * 4 + [anywhere] * 2,
        out_specs=[vmem] * 3,
        scratch_shapes=[
            pltpu.VMEM(full_qkv.shape, jnp.bfloat16),
            pltpu.VMEM(full_out.shape, jnp.bfloat16),
            pltpu.VMEM((CHUNKS, n, 2, 2, 2, share, width), jnp.bfloat16),
            pltpu.VMEM((CHUNKS, n, 2, 2, share, width), jnp.bfloat16),
            pltpu.VMEM((CHUNKS, n, 2, share, width), jnp.bfloat16),
            pltpu.VMEM((CHUNKS, n, share, width), jnp.bfloat16),
            pltpu.VMEM((CHUNKS, n - 1, share, width), jnp.bfloat16),
            pltpu.SemaphoreType.DMA((CHUNKS, kinds)),
            pltpu.SemaphoreType.DMA((CHUNKS, kinds)),
            pltpu.SemaphoreType.DMA((2,)),
        ],
        compiler_params=pltpu.CompilerParams(
            collective_id=1, has_side_effects=True, vmem_limit_bytes=54 << 20
        ),
        name="reduce_grads",
    )(tokens_t, cotangent_t, grad_qkv, mixed, full_qkv, full_out)


def attend_kernel(mask_ref, q_ref, k_ref, v_ref, gm_ref, mixed_ref, grad_ref):
    q, k, v, gm = q_ref[...], k_ref[...], v_ref[...], gm_ref[...]
    scale = q.shape[1] ** (-0.5)

    def dot(left, right, dims):
        return lax.dot_general(left, right, dims, preferred_element_type=jnp.float32)

    plain = (((1,), (0,)), ((), ()))
    scores = jnp.where(mask_ref[...] > 0.0, dot(q, k, CONTRACT_COLS) * scale, NEG_FILL)
    expvals = jnp.exp(scores - jnp.max(scores, axis=-1, keepdims=True))
    probs = expvals / jnp.sum(expvals, axis=-1, keepdims=True)
    probs_half = probs.astype(jnp.bfloat16)
    mixed_ref[...] = dot(probs_half, v, plain).astype(jnp.bfloat16)
    grad_probs = dot(gm, v, CONTRACT_COLS)
    inner = jnp.sum(probs * grad_probs, axis=-1, keepdims=True)
    grad_scores = (probs * (grad_probs - inner)).astype(jnp.bfloat16)
    grad_ref[0] = (dot(grad_scores, k, plain) * scale).astype(jnp.bfloat16)
    grad_ref[1] = (dot(grad_scores, q, CONTRACT_ROWS) * scale).astype(jnp.bfloat16)
    grad_ref[2] = dot(probs_half, gm, CONTRACT_ROWS).astype(jnp.bfloat16)


def attend(mask, qkv, grad_mixed, head_count):
    rows, width = grad_mixed.shape
    size = width // head_count

    def column(first):
        return pl.BlockSpec((rows, size), lambda h: (0, first + h))

    return pl.pallas_call(
        attend_kernel,
        grid=(head_count,),
        out_shape=[
            jax.ShapeDtypeStruct((rows, width), jnp.bfloat16),
            jax.ShapeDtypeStruct((3, rows, width), jnp.bfloat16),
        ],
        in_specs=[
            pl.BlockSpec((rows, rows), lambda h: (0, 0)),
            column(0),
            column(head_count),
            column(2 * head_count),
            column(0),
        ],
        out_specs=[column(0), pl.BlockSpec((3, rows, size), lambda h: (0, 0, h))],
        compiler_params=pltpu.CompilerParams(vmem_limit_bytes=48 << 20),
        name="attend",
    )(mask, qkv, qkv, qkv, grad_mixed)


def chip_body(tokens, w_qkv, w_out, doc_blocks, cotangent):
    row_count = tokens.shape[0]
    head_width = w_out.shape[1]
    n = lax.axis_size("fsdp")
    all_devices = lax.axis_size("dp") * n
    allowed = row_mask(doc_blocks[0], row_count)
    full_qkv, full_out, tokens_t, cotangent_t = gather_weights(
        n, w_qkv, w_out, tokens, cotangent
    )
    qkv = jnp.dot(tokens, full_qkv, preferred_element_type=jnp.float32).astype(jnp.bfloat16)
    grad_mixed = jnp.dot(cotangent, full_out, preferred_element_type=jnp.float32)
    grad_mixed = grad_mixed.astype(jnp.bfloat16)
    mixed, grad_qkv = attend(allowed.astype(jnp.float32), qkv, grad_mixed, H)
    summed, output, grad_tokens = reduce_grads(
        n, tokens_t, cotangent_t, grad_qkv, mixed, full_qkv, full_out
    )
    summed = summed.reshape(w_out.shape[0], 4 * head_width).astype(jnp.float32)
    norm_factor = 1.0 / math.sqrt(row_count * all_devices)
    grad_w_qkv = summed[:, : 3 * head_width] * norm_factor
    grad_w_out = summed[:, 3 * head_width :] * norm_factor
    return (output, grad_tokens, grad_w_qkv, grad_w_out)


def solution(mesh):
    placed = (
        P(("dp", "fsdp"), None),
        P("fsdp", None),
        P("fsdp", None),
        P(("dp", "fsdp"), None),
        P(("dp", "fsdp"), None),
    )
    in_plane = mesh.shape["dp"] == 8 and mesh.shape["fsdp"] == 4
    return jax.shard_map(
        chip_body if in_plane else body,
        mesh=mesh,
        in_specs=placed,
        out_specs=(
            P(("dp", "fsdp"), None),
            P(("dp", "fsdp"), None),
            P("fsdp", None),
            P("fsdp", None),
        ),
        check_vma=False,
    )
```
